32 devices in a mesh: src: 4 (over y, x), tgt: 8 (over z, core).
Axes of the slice: x: 2, y: 2, z: 4, core: 2. Of those that a mesh axis runs over, the one named last changes fastest.
Arguments:
- source_points: float32 [1024, 384], P('src'), as said below
- target_points: float32 [6144, 384], P('tgt'), as said below
- plan_start: float32 [1024, 6144], P('src', 'tgt'), may hold values from 0.06 to 140, as said below
- source_mass: float32 [1024], P('src'), may hold values from 0.3 to 3
- target_mass: float32 [6144], P('tgt'), may hold values from 0.3 to 3
- epsilon: float32 [1], replicated, may hold values from 0.5 to 1
Outputs:
- transported: float32 [1024, 384], P(('src', 'tgt'))
- core: float32 [384, 384], replicated
- column_scale: float32 [6144], P('tgt')
The draws below stay inside these ranges and needn't reach their ends.
Inputs may be any that keep to these rules, and one draw needn't show every extreme that they name: `source_points`: real-valued features. `target_points`: real-valued features. `plan_start`: positive entries.
All inputs are finite; a program needn't handle non-finite values.
Results may differ from the reference program's by a relative error of at most 0.00011.
Values sent between devices are 32-bit elements; how exact they have to be, the bound alone decides.
No kernel may reach another device: no remote copies, remote signals or barrier semaphores. Data moves between devices by JAX's collectives and lax.ppermute only.
A program may use at most 64 MiB of HBM per device.

```python
import math
import jax
import jax.numpy as jnp
from jax import lax

D = 384
ITERS = 2
SOURCES = 1024
TARGETS = 6144


def shared_fields(key):
    base = jax.random.fold_in(key, 7101)
    keys = jax.random.split(base, 7)
    latent_src = jnp.clip(jax.random.normal(keys[0], (SOURCES, D), jnp.float32), -3.0, 3.0)
    latent_tgt = jnp.clip(jax.random.normal(keys[1], (TARGETS, D), jnp.float32), -3.0, 3.0)
    mixing_src = jnp.eye(D, dtype=jnp.float32) + 0.6 * jax.random.normal(keys[2], (D, D), jnp.float32) / math.sqrt(1.0 * D)
    mixing_tgt = jnp.eye(D, dtype=jnp.float32) + 0.6 * jax.random.normal(keys[3], (D, D), jnp.float32) / math.sqrt(1.0 * D)
    points_src = 0.5 * jnp.dot(latent_src, mixing_src)
    points_tgt = 0.5 * jnp.dot(latent_tgt, mixing_tgt)
    similar = jnp.clip(jnp.dot(latent_src, latent_tgt.T) / math.sqrt(1.0 * D), -4.0, 4.0)
    rough = jnp.exp(jax.random.uniform(keys[6], (SOURCES, TARGETS), jnp.float32, math.log(0.5), math.log(2.0)))
    row_rise = jnp.exp(math.log(3.0) * jnp.arange(SOURCES, dtype=jnp.float32) / SOURCES)
    col_rise = jnp.exp(math.log(3.0) * jnp.arange(TARGETS, dtype=jnp.float32) / TARGETS)
    plan = rough * jnp.exp(0.5 * similar) * row_rise[:, None] * col_rise[None, :]
    return (points_src, points_tgt, plan)


def draw_source_points(key, part):
    return shared_fields(key)[0]


def draw_target_points(key, part):
    return shared_fields(key)[1]


def draw_plan_start(key, part):
    return shared_fields(key)[2]


def shard_levels(key, shape, pieces, low, top_value):
    factor_of = 1.0
    for axis_at, blocks in pieces:
        draws = jax.random.uniform(jax.random.fold_in(jax.random.fold_in(key, 6), axis_at), (blocks,), jnp.float32, low / len(pieces), top_value / len(pieces))
        factor_of = factor_of * jnp.repeat(jnp.exp(draws), shape[axis_at] // blocks).reshape((-1,) + (1,) * (len(shape) - 1 - axis_at))
    return factor_of


def setup_inputs(seed: int = 0) -> dict:
    key_list = jax.random.split(jax.random.key(seed), 7)
    source_points = draw_source_points(jax.random.fold_in(key_list[6], 71), 0)
    target_points = draw_target_points(jax.random.fold_in(key_list[6], 71), 0)
    plan_start = draw_plan_start(jax.random.fold_in(key_list[6], 71), 0)
    source_mass = jnp.clip(jnp.exp(math.log(3.0) - 2.3025851 * jax.random.uniform(key_list[3], (SOURCES,), jnp.float32) ** shard_levels(key_list[3], (SOURCES,), ((0, 4),), -0.2, 0.2)), 0.3, 3.0)
    target_mass = jnp.clip(jnp.exp(math.log(3.0) - 2.3025851 * jax.random.uniform(key_list[4], (TARGETS,), jnp.float32) ** shard_levels(key_list[4], (TARGETS,), ((0, 8),), -0.2, 0.2)), 0.3, 3.0)
    epsilon = jnp.clip(jax.random.uniform(key_list[5], (1,), jnp.float32, 0.5, 1.0), 0.5, 1.0)
    return dict(source_points=source_points, target_points=target_points, plan_start=plan_start, source_mass=source_mass, target_mass=target_mass, epsilon=epsilon)


def product(left, right):
    return jnp.dot(left, right, precision=lax.Precision.HIGHEST, preferred_element_type=jnp.float32)


def reference(source_points, target_points, plan_start, source_mass, target_mass, epsilon):
    moved = product(plan_start, target_points)
    core = product(source_points.T, moved) / (SOURCES * TARGETS)
    affinity = product(product(source_points, core), target_points.T)
    kernel = plan_start * jnp.exp(2.0 * affinity / epsilon[0])
    column_scale = jnp.ones((TARGETS,), jnp.float32)
    row_scale = jnp.ones((SOURCES,), jnp.float32)
    for sweep in range(ITERS):
        row_scale = source_mass / product(kernel, column_scale)
        column_scale = target_mass / product(row_scale, kernel)
    weighted = kernel * row_scale[:, None] * column_scale[None, :]
    transported = product(weighted, target_points) / source_mass[:, None]
    return transported, core, column_scale
```

```python
import jax
import jax.numpy as jnp
from jax import lax
from jax.sharding import PartitionSpec as P

ITERS = 2


def product(left, right):
    return jnp.dot(left, right, precision=lax.Precision.HIGHEST, preferred_element_type=jnp.float32)


def digits(size, first):
    found, stride = [], 1
    while stride < size:
        left = size // stride
        radix = first if (stride == 1 and first) else (4 if left % 4 == 0 else 2)
        found.append((stride, radix))
        stride *= radix
    return found


def swap(value, axis, stride, k):
    size = lax.axis_size(axis)
    return lax.ppermute(value, axis, [(i, i ^ (k * stride)) for i in range(size)])


def digit_of(axis, stride, radix):
    return (lax.axis_index(axis) // stride) % radix


def total(value, axis, stride, radix):
    parts = [value] + [swap(value, axis, stride, k) for k in range(1, radix)]
    while len(parts) > 1:
        parts = [parts[i] + parts[i + 1] for i in range(0, len(parts), 2)]
    return parts[0]


def scatter(blocks, axis, stride, radix):
    mine = digit_of(axis, stride, radix)
    split = blocks.reshape((blocks.shape[0] // radix, radix) + blocks.shape[1:])

    def pick(at):
        return lax.dynamic_index_in_dim(split, at, 1, keepdims=False)

    parts = [swap(pick(mine ^ k), axis, stride, k) for k in range(1, radix)]
    value = pick(mine)
    for part in parts:
        value = value + part
    return value


def gather(blocks, axis, stride, radix):
    mine = digit_of(axis, stride, radix)
    whole = jnp.zeros((blocks.shape[0], radix) + blocks.shape[1:], blocks.dtype)
    parts = [swap(blocks, axis, stride, k) for k in range(1, radix)]
    for k, part in enumerate([blocks] + parts):
        whole = lax.dynamic_update_index_in_dim(whole, part, mine ^ k, 1)
    return whole.reshape((blocks.shape[0] * radix,) + blocks.shape[1:])


def per_device(source_points, target_points, plan_start, source_mass, target_mass, epsilon):
    n_src, n_tgt = lax.axis_size("src"), lax.axis_size("tgt")
    total_items = source_points.shape[0] * n_src * target_points.shape[0] * n_tgt
    width = source_points.shape[1]
    src_digits = digits(n_src, 0)
    tgt_digits = digits(n_tgt, 2)

    moved = product(plan_start, target_points)
    part = product(source_points.T, moved)
    pieces = tgt_digits[0][1] * n_src
    blocks = part.reshape(pieces, width // pieces, width)
    path = [("tgt",) + tgt_digits[0]] + [("src",) + d for d in src_digits]
    for step in path:
        blocks = scatter(blocks, *step)
    for d in tgt_digits[1:]:
        blocks = total(blocks, "tgt", *d)
    for step in reversed(path):
        blocks = gather(blocks, *step)
    core = blocks.reshape(width, width) / total_items

    affinity = product(product(source_points, core), target_points.T)
    kernel = plan_start * jnp.exp(2.0 * affinity / epsilon[0])
    column_scale = jnp.ones((target_points.shape[0],), jnp.float32)
    row_scale = jnp.ones((source_points.shape[0],), jnp.float32)
    for sweep in range(ITERS):
        row_total = product(kernel, column_scale)
        for d in tgt_digits:
            row_total = total(row_total, "tgt", *d)
        row_scale = source_mass / row_total
        column_total = product(row_scale, kernel)
        for d in src_digits:
            column_total = total(column_total, "src", *d)
        column_scale = target_mass / column_total
    weighted = kernel * row_scale[:, None] * column_scale[None, :]
    share = product(weighted, target_points) / source_mass[:, None]
    blocks = share.reshape(n_tgt, share.shape[0] // n_tgt, width)
    for d in tgt_digits:
        blocks = scatter(blocks, "tgt", *d)
    transported = blocks.reshape(share.shape[0] // n_tgt, width)
    return (transported, core, column_scale)


def solution(mesh):
    placed = (P("src", None), P("tgt", None), P("src", "tgt"), P("src"), P("tgt"), P())
    return jax.shard_map(
        per_device,
        mesh=mesh,
        in_specs=placed,
        out_specs=(P(("src", "tgt"), None), P(), P("tgt")),
        check_vma=False,
    )
```
